32 devices in a mesh: grp: 2 (over x), row: 4 (over y, core), col: 4 (over z).
Axes of the slice: x: 2, y: 2, z: 4, core: 2. Of those that a mesh axis runs over, the one named last changes fastest.
Arguments:
- gradients: bfloat16 [2, 3072, 24576], P('grp', 'row', 'col'), may hold values from -6 to 6
- momentum: float32 [2, 3072, 24576], P('grp', 'row', 'col'), may hold values from -94 to 94, as said below
- right_basis: bfloat16 [24576, 512], P('col'), may hold values from -6 to 6
Outputs:
- new_momentum: float32 [2, 3072, 24576], P('grp', 'row', 'col')
- new_basis: bfloat16 [24576, 512], P('col')
- update: bfloat16 [3072, 24576], P('row', 'col')
The draws below stay inside these ranges and needn't reach their ends.
Inputs may be any that keep to these rules, and one draw needn't show every extreme that they name: Each group's momentum buffer holds real values bounded in magnitude by 94.
All inputs are finite; a program needn't handle non-finite values.
Results may differ from the reference program's by a relative error of at most 0.013.
Values may be sent and summed in bfloat16 or wider, within the bound.
No kernel may reach another device: no remote copies, remote signals or barrier semaphores. Data moves between devices by JAX's collectives and lax.ppermute only.
A program may use at most 192 MiB of HBM per device.

```python
import math
import jax
import jax.numpy as jnp
from jax import lax

D = 3072
FF = 24576
R = 512
GROUPS = 2


def draw_momentum(key, part):
    keys = jax.random.split(jax.random.fold_in(key, 17), 4)
    row_scale = jnp.exp(jax.random.uniform(keys[0], (D,), jnp.float32, math.log(0.3), math.log(3.0)))
    position = jnp.arange(FF, dtype=jnp.float32) / FF
    col_scale = jnp.exp(jax.random.uniform(keys[1], (FF,), jnp.float32, math.log(0.3), math.log(3.0))) * jnp.exp(math.log(3.0) * (position - 0.5))
    common = jax.random.normal(keys[2], (1, D, FF), jnp.float32)
    own = jax.random.normal(keys[3], (GROUPS, D, FF), jnp.float32)
    mixed = 0.8 * common + 0.6 * own
    mixed = jnp.clip(mixed, -6.0, 6.0)
    return (mixed * row_scale[None, :, None] * col_scale[None, None, :]).astype(jnp.float32)


def block_levels(key, extent, cuts, low, largest):
    factor_of = 1.0
    for dim, parts in cuts:
        draws = jax.random.uniform(jax.random.fold_in(jax.random.fold_in(key, 6), dim), (parts,), jnp.float32, low / len(cuts), largest / len(cuts))
        factor_of = factor_of * jnp.repeat(jnp.exp(draws), extent[dim] // parts).reshape((-1,) + (1,) * (len(extent) - 1 - dim))
    return factor_of


def gaussian(key, dims, spread, bound, cuts=(), kind=jnp.bfloat16):
    result = jax.random.normal(key, dims, jnp.float32) * spread
    if len(cuts) > 0:
        result = block_levels(key, dims, cuts, -0.22, 0.18) * result
    return jnp.clip(result, min=-bound, max=bound).astype(kind)


def setup_inputs(seed: int = 0) -> dict:
    seeds = jax.random.split(jax.random.key(seed), 4)
    return {
        "gradients": gaussian(seeds[0], (GROUPS, D, FF), 1.0, 6.0, ((0, 2), (1, 4), (2, 4))),
        "momentum": draw_momentum(jax.random.fold_in(seeds[3], 71), 0),
        "right_basis": gaussian(seeds[2], (FF, R), 1.0, 6.0, ((0, 4),)),
    }


momentum_decay = 0.9
ridge_scale = 0.0001
epsilon = 1e-06

def reference(gradients, momentum, right_basis):
    left_factor = jnp.zeros((D, R), jnp.float32)
    for group in range(GROUPS):
        merged_low = (momentum[group] + gradients[group].astype(jnp.float32)).astype(jnp.bfloat16)
        left_factor = left_factor + jnp.dot(merged_low.astype(jnp.float32), right_basis.astype(jnp.float32), preferred_element_type=jnp.float32)
    gram_matrix = jnp.dot(left_factor.T.astype(jnp.float32), left_factor.astype(jnp.float32), precision=lax.Precision.HIGHEST, preferred_element_type=jnp.float32)
    shifted = gram_matrix + ridge_scale * (jnp.trace(gram_matrix) / R) * jnp.eye(R, dtype=jnp.float32)
    cholesky_factor = jnp.linalg.cholesky(shifted)
    orthonormal = jax.scipy.linalg.solve_triangular(cholesky_factor, left_factor.T, lower=True).T
    orthonormal_low = orthonormal.astype(jnp.bfloat16)
    right_factor = jnp.zeros((FF, R), jnp.float32)
    for group in range(GROUPS):
        merged_low = (momentum[group] + gradients[group].astype(jnp.float32)).astype(jnp.bfloat16)
        right_factor = right_factor + jnp.dot(merged_low.T.astype(jnp.float32), orthonormal_low.astype(jnp.float32), preferred_element_type=jnp.float32)
    right_factor = right_factor / GROUPS
    column_rms = jnp.sqrt(lax.optimization_barrier(jnp.sum(right_factor * right_factor, axis=0)) / FF + epsilon)
    new_basis = (right_factor / column_rms).astype(jnp.bfloat16)
    scaled_low = (orthonormal * column_rms).astype(jnp.bfloat16)
    update = (math.sqrt(D / R) * jnp.dot(orthonormal_low.astype(jnp.float32), new_basis.T.astype(jnp.float32), preferred_element_type=jnp.float32)).astype(jnp.bfloat16)
    feedback = jnp.dot(scaled_low.astype(jnp.float32), new_basis.T.astype(jnp.float32), preferred_element_type=jnp.float32)
    outputs = []
    for group in range(GROUPS):
        merged = momentum[group] + gradients[group].astype(jnp.float32)
        outputs.append(merged - (1 - momentum_decay) * feedback)
    return (jnp.stack(outputs), new_basis, update)
```

```python
import math

import jax
import jax.numpy as jnp
from jax import lax
from jax.experimental import pallas as pl
from jax.experimental.pallas import tpu as pltpu
from jax.sharding import PartitionSpec as P

momentum_decay = 0.9
ridge_scale = 0.0001
epsilon = 1e-06

F32 = jnp.float32
BF16 = jnp.bfloat16
HIGHEST = lax.Precision.HIGHEST
LANES = 128


def dot(a, b, dims, precision=None):
    return lax.dot_general(a, b, (dims, ((), ())), precision=precision, preferred_element_type=F32)


def swap(value, axis, bit):
    return lax.ppermute(value, axis, [(i, i ^ bit) for i in range(lax.axis_size(axis))])


def left_kernel(table, grad_ref, mom_ref, basis_ref, low_ref, out_ref, acc):
    step = pl.program_id(0)
    low = (mom_ref[0] + grad_ref[0].astype(F32)).astype(BF16)
    low_ref[...] = low
    part = dot(low, basis_ref[...], ((1,), (0,)))

    @pl.when(step == 0)
    def _():
        acc[...] = part

    @pl.when(step > 0)
    def _():
        acc[...] += part

    @pl.when(step == pl.num_programs(0) - 1)
    def _():
        out_ref[...] = acc[...].astype(out_ref.dtype)


def left_product(half, gradients, momentum, right_basis, dtype, low=None):
    _, rows, cols = momentum.shape
    rank = right_basis.shape[1]
    rows //= 2
    width = 512
    row_block = lambda k, t: (0, t[0], k)
    outs = (jax.ShapeDtypeStruct((2 * rows, cols), BF16), jax.ShapeDtypeStruct((rows, rank), dtype))
    operands = [half, gradients, momentum, right_basis]
    in_specs = [
        pl.BlockSpec((1, rows, width), row_block),
        pl.BlockSpec((1, rows, width), row_block),
        pl.BlockSpec((width, rank), lambda k, t: (k, 0)),
    ]
    kernel, aliases = left_kernel, {}
    if low is not None:
        operands.append(low)
        in_specs.append(pl.BlockSpec(memory_space=pl.ANY))
        aliases = {4: 0}
        kernel = lambda t, a, b, c, _, *rest: left_kernel(t, a, b, c, *rest)
    return pl.pallas_call(
        kernel,
        out_shape=outs,
        grid_spec=pltpu.PrefetchScalarGridSpec(
            num_scalar_prefetch=1,
            grid=(cols // width,),
            in_specs=in_specs,
            out_specs=(
                pl.BlockSpec((rows, width), lambda k, t: (t[0], k)),
                pl.BlockSpec((rows, rank), lambda k, t: (0, 0)),
            ),
            scratch_shapes=[pltpu.VMEM((rows, rank), F32)],
        ),
        input_output_aliases=aliases,
        cost_estimate=pl.CostEstimate(
            flops=2 * rows * cols * rank, transcendentals=0, bytes_accessed=8 * rows * cols + 2 * cols * rank
        ),
        name="left_product",
    )(*operands)


def right_kernel(table, left_ref, low_ref, *refs):
    part = dot(left_ref[...], low_ref[...], ((1,), (0,)))
    if len(refs) == 2:
        part = part + refs[0][...].astype(F32)
    refs[-1][...] = part.astype(refs[-1].dtype)


def right_product(blocks, left_t, low, dtype, received=None):
    rank, rows = left_t.shape
    count = blocks.shape[0]
    width = low.shape[1] // 16
    operands = [blocks, left_t, low]
    in_specs = [
        pl.BlockSpec((rank, rows), lambda k, t: (0, 0)),
        pl.BlockSpec((rows, width), lambda k, t: (0, t[k])),
    ]
    if received is not None:
        operands.append(received)
        in_specs.append(pl.BlockSpec((rank, width), lambda k, t: (0, k)))
    return pl.pallas_call(
        right_kernel,
        out_shape=jax.ShapeDtypeStruct((rank, count * width), dtype),
        grid_spec=pltpu.PrefetchScalarGridSpec(
            num_scalar_prefetch=1,
            grid=(count,),
            in_specs=in_specs,
            out_specs=pl.BlockSpec((rank, width), lambda k, t: (0, k)),
        ),
        cost_estimate=pl.CostEstimate(
            flops=2 * rank * rows * count * width,
            transcendentals=0,
            bytes_accessed=2 * count * width * (rows + 2 * rank),
        ),
        name="right_product",
    )(*operands)


def invert_block(block, size):
    lane = lax.broadcasted_iota(jnp.int32, (size, size), 1)
    sub = lax.broadcasted_iota(jnp.int32, (size, size), 0)
    lane8 = lax.broadcasted_iota(jnp.int32, (8, size), 1)
    sub8 = lax.broadcasted_iota(jnp.int32, (8, size), 0)
    rows = [block[8 * v : 8 * v + 8, :] for v in range(size // 8)]
    for j in range(size):
        first, at = j // 8, j % 8
        pivot_row = rows[first][at : at + 1, :]
        inverse = 1.0 / pivot_row[:, j : j + 1]
        scaled = jnp.where(lane8 == j, inverse, jnp.broadcast_to(pivot_row * inverse, (8, size)))
        for v in range(first, size // 8):
            row = rows[v]
            column = row[:, j : j + 1]
            if v > first:
                rows[v] = jnp.where(lane8 == j, 0.0, row) - column * scaled
            elif at < 7:
                column = jnp.where(sub8[:, :1] > at, column, 0.0)
                rows[v] = jnp.where((lane8 == j) & (sub8 > at), 0.0, row) - column * scaled
    done = jnp.concatenate(rows, 0)
    pivots = jnp.sum(jnp.where(lane == sub, done, 0.0), axis=1, keepdims=True)
    return jnp.where(lane < sub, done, jnp.where(lane == sub, 1.0, 0.0)) * lax.rsqrt(pivots)


def inverse_factor_kernel(gram_ref, out_ref, work, *, size):
    n = gram_ref.shape[0]
    gram = gram_ref[...]
    diagonal = lax.broadcasted_iota(jnp.int32, (n, n), 0) == lax.broadcasted_iota(jnp.int32, (n, n), 1)
    trace = jnp.sum(jnp.where(diagonal, gram, 0.0))
    work[...] = gram + jnp.where(diagonal, ridge_scale * (trace / n), 0.0)
    out_ref[...] = jnp.zeros_like(out_ref)
    for k in range(n // size):
        here, before = slice(k * size, (k + 1) * size), slice(0, k * size)
        upto, after = slice(0, (k + 1) * size), slice((k + 1) * size, n)
        inverse = invert_block(work[here, here], size)
        out_ref[here, here] = inverse
        if k > 0:
            out_ref[here, before] = dot(inverse, out_ref[here, before], ((1,), (0,)), HIGHEST)
        if (k + 1) * size < n:
            factor = dot(work[after, here], inverse, ((1,), (1,)), HIGHEST)
            work[after, after] -= dot(factor, factor, ((1,), (1,)), HIGHEST)
            out_ref[after, upto] -= dot(factor, out_ref[here, upto], ((1,), (0,)), HIGHEST)


def inverse_factor(gram):
    n = gram.shape[0]
    return pl.pallas_call(
        lambda *refs: inverse_factor_kernel(*refs, size=LANES),
        out_shape=jax.ShapeDtypeStruct((n, n), F32),
        scratch_shapes=[pltpu.VMEM((n, n), F32)],
        cost_estimate=pl.CostEstimate(flops=40 * 10**9, transcendentals=0, bytes_accessed=8 * n * n),
        name="inverse_factor",
    )(gram)


def finish_kernel(inverse_ref, first_ref, second_ref, out_ref, squares_ref, *, scale):
    width = first_ref.shape[1]
    inverse = inverse_ref[...]
    high = inverse.astype(BF16)
    low = (inverse - high.astype(F32)).astype(BF16)
    total = jnp.zeros((inverse.shape[0], 1), F32)
    for at, ref in ((0, first_ref), (width, second_ref)):
        value = ref[...] * scale
        value_high = value.astype(BF16)
        value_low = (value - value_high.astype(F32)).astype(BF16)
        piece = (
            dot(high, value_high, ((1,), (0,)))
            + dot(low, value_high, ((1,), (0,)))
            + dot(high, value_low, ((1,), (0,)))
        )
        total = total + jnp.sum(piece * piece, axis=1, keepdims=True)
        out_ref[:, at : at + width] = piece.astype(out_ref.dtype)
    squares_ref[...] = jnp.broadcast_to(total, squares_ref.shape)


def finish_piece(inverse, first, second, scale):
    rank, width = first.shape
    return pl.pallas_call(
        lambda *refs: finish_kernel(*refs, scale=scale),
        out_shape=(
            jax.ShapeDtypeStruct((rank, 2 * width), BF16),
            jax.ShapeDtypeStruct((rank, LANES), F32),
        ),
        name="finish_piece",
    )(inverse, first, second)


def orthonormal_kernel(left_ref, inverse_ref, out_ref):
    inverse = inverse_ref[...]
    high = inverse.astype(BF16)
    low = (inverse - high.astype(F32)).astype(BF16)
    left = left_ref[...]
    out_ref[...] = dot(left, high, ((1,), (1,))) + dot(left, low, ((1,), (1,)))


def orthonormal_rows(left, inverse):
    return pl.pallas_call(
        orthonormal_kernel,
        out_shape=jax.ShapeDtypeStruct(left.shape, F32),
        name="orthonormal_rows",
    )(left, inverse)


def output_kernel(table, inverse_rms_ref, ortho_ref, scaled_ref, mom_ref, grad_ref, right_ref, *refs, scale):
    mom_out, basis_out, update_out = refs[-3:]
    basis = (right_ref[...].astype(F32) * inverse_rms_ref[:, :1]).astype(BF16)
    basis_out[...] = basis.T
    update_out[...] = (scale * dot(ortho_ref[...], basis, ((1,), (0,)))).astype(BF16)
    feedback = dot(scaled_ref[...], basis, ((1,), (0,)))
    mom_out[0] = mom_ref[0] + grad_ref[0].astype(F32) - (1 - momentum_decay) * feedback


def write_outputs(blocks, inverse_rms, ortho, scaled, momentum, gradients, piece, scale, previous):
    _, rows, cols = momentum.shape
    rank = ortho.shape[1]
    width = cols // 16
    count = piece.shape[1] // width
    whole = lambda k, t: (0, 0)
    local = lambda k, t: (0, 0, t[k])
    operands = [blocks, inverse_rms, ortho, scaled, momentum, gradients, piece]
    in_specs = [
        pl.BlockSpec((rank, LANES), whole),
        pl.BlockSpec((rows, rank), whole),
        pl.BlockSpec((rows, rank), whole),
        pl.BlockSpec((1, rows, width), local),
        pl.BlockSpec((1, rows, width), local),
        pl.BlockSpec((rank, width), lambda k, t: (0, k)),
    ]
    aliases = {}
    if previous is not None:
        aliases = {len(operands) + i: i for i in range(3)}
        operands += list(previous)
        in_specs += [pl.BlockSpec(memory_space=pl.ANY)] * 3
    return pl.pallas_call(
        lambda *refs: output_kernel(*refs, scale=scale),
        out_shape=(
            jax.ShapeDtypeStruct((1, rows, cols), F32),
            jax.ShapeDtypeStruct((cols, rank), BF16),
            jax.ShapeDtypeStruct((rows, cols), BF16),
        ),
        grid_spec=pltpu.PrefetchScalarGridSpec(
            num_scalar_prefetch=1,
            grid=(count,),
            in_specs=in_specs,
            out_specs=(
                pl.BlockSpec((1, rows, width), local),
                pl.BlockSpec((width, rank), lambda k, t: (t[k], 0)),
                pl.BlockSpec((rows, width), lambda k, t: (0, t[k])),
            ),
        ),
        input_output_aliases=aliases,
        cost_estimate=pl.CostEstimate(
            flops=4 * rows * rank * width * count, transcendentals=0, bytes_accessed=14 * rows * width * count
        ),
        name="write_outputs",
    )(*operands)


def by_pieces(gradients, momentum, right_basis):
    _, local_rows, local_cols = momentum.shape
    rank = right_basis.shape[1]
    groups, cols = lax.axis_size("grp"), lax.axis_size("col")
    model_rows = local_rows * lax.axis_size("row")
    model_cols = local_cols * cols
    x, row, z = lax.axis_index("grp"), lax.axis_index("row"), lax.axis_index("col")
    y, core = row // 2, row % 2

    theirs = jnp.reshape(1 - x, (1,)).astype(jnp.int32)
    mine = jnp.reshape(x, (1,)).astype(jnp.int32)
    low, left_theirs = left_product(theirs, gradients, momentum, right_basis, BF16)
    left_from_x = swap(left_theirs, "grp", 1)
    low, left_mine = left_product(mine, gradients, momentum, right_basis, F32, low)
    half = (left_mine + left_from_x.astype(F32)).reshape(cols, -1, rank)
    pick = lambda s: lax.dynamic_index_in_dim(half, z ^ s, 0, keepdims=False)
    piece = pick(0)
    for s in range(1, cols):
        piece = piece + swap(pick(s).astype(BF16), "col", s).astype(F32)
    piece = piece.astype(BF16)
    parts = jnp.stack([piece] + [swap(piece, "col", s) for s in range(1, cols)])
    half = jnp.take(parts, jnp.arange(cols) ^ z, axis=0).reshape(-1, rank)
    other = swap(half, "grp", 1)
    left = jnp.where(x == 0, jnp.concatenate([half, other]), jnp.concatenate([other, half]))
    left_t = left.T

    gram = dot(left, left, ((0,), (0,)))
    h, q = rank // 2, rank // 4
    packs = [
        jnp.concatenate([gram[:h, :h], gram[h : h + q, :h]]),
        jnp.concatenate([gram[h:, h:], gram[h + q :, :h]]),
    ]
    keep = jnp.where(core == 0, packs[0], packs[1])
    give = jnp.where(core == 0, packs[1], packs[0])
    keep = keep + swap(give, "row", 1)
    keep = keep + swap(keep, "row", 2)
    got = swap(keep, "row", 1)
    pack0 = jnp.where(core == 0, keep, got)
    pack1 = jnp.where(core == 0, got, keep)
    cross = jnp.concatenate([pack0[h:], pack1[h:]])
    gram = jnp.concatenate(
        [jnp.concatenate([pack0[:h], cross.T], axis=1), jnp.concatenate([cross, pack1[:h]], axis=1)]
    )
    inverse = inverse_factor(gram)

    def block(part, dc, dx, dy):
        return ((core ^ dc) * 4 + (x ^ dx) * 2 + (y ^ dy)) * 2 + part

    def table(items):
        return jnp.stack([block(*item) for item in items]).astype(jnp.int32)

    def halves(dc):
        return (
            [(0, dc, 1, 1), (0, dc, 1, 0)],
            [(1, dc, 1, 1), (1, dc, 0, 1)],
            [(0, dc, 0, 1), (0, dc, 0, 0), (1, dc, 1, 0), (1, dc, 0, 0)],
        )

    given = [right_product(table(items), left_t, low, BF16) for items in halves(1)]
    got = [swap(value, "row", 1) for value in given]
    types = (BF16, BF16, F32)
    sums = [right_product(table(i), left_t, low, t, r) for i, t, r in zip(halves(0), types, got)]
    width = local_cols // 16
    from_x = swap(sums[0], "grp", 1).astype(F32)
    from_y = swap(sums[1], "row", 2).astype(F32)
    rest = sums[2]
    first_y = rest[:, :width] + from_x[:, :width]
    first = rest[:, width : 2 * width] + from_x[:, width:]
    second_x = rest[:, 2 * width : 3 * width] + from_y[:, :width]
    second = rest[:, 3 * width :] + from_y[:, width:]
    first = first + swap(first_y.astype(BF16), "row", 2).astype(F32)
    second = second + swap(second_x.astype(BF16), "grp", 1).astype(F32)
    piece, squares = finish_piece(inverse, first, second, 1.0 / groups)

    squares = squares[:, 0]
    for axis, bits in (("col", (1, 2)), ("grp", (1,)), ("row", (2, 1))):
        for bit in bits:
            squares = squares + swap(squares, axis, bit)
    column_rms = jnp.sqrt(squares / model_cols + epsilon)
    ortho = orthonormal_rows(left, inverse)
    scaled = (ortho * column_rms).astype(BF16)
    ortho = ortho.astype(BF16)
    inverse_rms = jnp.broadcast_to((1.0 / column_rms)[:, None], (rank, LANES))

    piece_c = swap(piece, "row", 1)
    piece_x = swap(piece, "grp", 1)
    piece_y = swap(piece, "row", 2)
    diagonal = jnp.concatenate([swap(piece_y[:, :width], "grp", 1), swap(piece_x[:, width:], "row", 2)], axis=1)
    piece_xc, piece_yc = swap(piece_x, "row", 1), swap(piece_y, "row", 1)
    diagonal_c = swap(diagonal, "row", 1)
    outputs = None
    for dx, dy, pair in ((0, 0, (piece, piece_c)), (1, 0, (piece_x, piece_xc)), (0, 1, (piece_y, piece_yc)), (1, 1, (diagonal, diagonal_c))):
        for dc, value in enumerate(pair):
            blocks = table([(part, dc, dx, dy) for part in range(2)])
            outputs = write_outputs(
                blocks, inverse_rms, ortho, scaled, momentum, gradients, value, math.sqrt(model_rows / rank), outputs
            )
    return outputs


def by_collectives(gradients, momentum, right_basis):
    merged = momentum[0] + gradients[0].astype(F32)
    merged_low = merged.astype(BF16)
    rank = right_basis.shape[1]
    local_rows, local_cols = merged.shape
    model_rows = local_rows * lax.axis_size("row")
    model_cols = local_cols * lax.axis_size("col")
    groups = lax.axis_size("grp")
    left_factor = jnp.dot(merged_low, right_basis, preferred_element_type=F32)
    left_factor = lax.psum(left_factor, ("grp", "col"))
    gram_matrix = dot(left_factor, left_factor, ((0,), (0,)), HIGHEST)
    gram_matrix = lax.psum(gram_matrix, "row")
    shifted = gram_matrix + ridge_scale * (jnp.trace(gram_matrix) / rank) * jnp.eye(rank, dtype=F32)
    cholesky_factor = jnp.linalg.cholesky(shifted)
    orthonormal = jax.scipy.linalg.solve_triangular(cholesky_factor, left_factor.T, lower=True).T
    orthonormal_low = orthonormal.astype(BF16)
    right_piece = lax.psum_scatter(
        jnp.einsum("ij,ik->jk", merged_low, orthonormal_low, preferred_element_type=F32) / groups,
        ("grp", "row"),
        scatter_dimension=0,
        tiled=True,
    )
    squares_sum = lax.psum(jnp.sum(right_piece * right_piece, axis=0), ("grp", "row", "col"))
    column_rms = jnp.sqrt(squares_sum / model_cols + epsilon)
    basis_piece = (right_piece / column_rms).astype(BF16)
    new_basis = lax.all_gather(basis_piece, ("grp", "row"), axis=0, tiled=True)
    scaled_low = (orthonormal * column_rms).astype(BF16)
    stacked_left = jnp.concatenate([orthonormal_low, scaled_low], axis=0)
    products = dot(stacked_left, new_basis, ((1,), (1,)))
    update = (math.sqrt(model_rows / rank) * products[:local_rows]).astype(BF16)
    new_momentum = merged - (1 - momentum_decay) * products[local_rows:]
    return (new_momentum[None], new_basis, update)


def solution(mesh):
    placed = (P("grp", "row", "col"), P("grp", "row", "col"), P("col", None))

    def per_device(gradients, momentum, right_basis):
        _, rows, cols = momentum.shape
        rank = right_basis.shape[1]
        fits = (
            mesh.shape["grp"] == 2
            and mesh.shape["row"] == 4
            and mesh.shape["col"] == 4
            and rows % LANES == 0
            and cols % (16 * LANES) == 0
            and cols % 512 == 0
            and rank % (4 * LANES) == 0
        )
        return (by_pieces if fits else by_collectives)(gradients, momentum, right_basis)

    return jax.shard_map(
        per_device,
        mesh=mesh,
        in_specs=placed,
        out_specs=(P("grp", "row", "col"), P("col", None), P("row", "col")),
        check_vma=False,
    )
```

```python
import math

import jax
import jax.numpy as jnp
from jax import lax
from jax.experimental import pallas as pl
from jax.experimental.pallas import tpu as pltpu
from jax.sharding import PartitionSpec as P

momentum_decay = 0.9
ridge_scale = 0.0001
epsilon = 1e-06

F32 = jnp.float32
BF16 = jnp.bfloat16
HIGHEST = lax.Precision.HIGHEST
LANES = 128


def dot(a, b, dims, precision=None):
    return lax.dot_general(a, b, (dims, ((), ())), precision=precision, preferred_element_type=F32)


def swap(value, axis, bit):
    return lax.ppermute(value, axis, [(i, i ^ bit) for i in range(lax.axis_size(axis))])


def left_kernel(table, grad_ref, mom_ref, basis_ref, low_ref, out_ref, acc):
    step = pl.program_id(0)
    low = (mom_ref[0] + grad_ref[0].astype(F32)).astype(BF16)
    low_ref[...] = low
    part = dot(low, basis_ref[...], ((1,), (0,)))

    @pl.when(step == 0)
    def _():
        acc[...] = part

    @pl.when(step > 0)
    def _():
        acc[...] += part

    @pl.when(step == pl.num_programs(0) - 1)
    def _():
        out_ref[...] = acc[...].astype(out_ref.dtype)


def left_product(half, gradients, momentum, right_basis, dtype, low=None):
    _, rows, cols = momentum.shape
    rank = right_basis.shape[1]
    rows //= 2
    width = math.gcd(cols, 1024)
    row_block = lambda k, t: (0, t[0], k)
    outs = (jax.ShapeDtypeStruct((2 * rows, cols), BF16), jax.ShapeDtypeStruct((rows, rank), dtype))
    operands = [half, gradients, momentum, right_basis]
    in_specs = [
        pl.BlockSpec((1, rows, width), row_block),
        pl.BlockSpec((1, rows, width), row_block),
        pl.BlockSpec((width, rank), lambda k, t: (k, 0)),
    ]
    kernel, aliases = left_kernel, {}
    if low is not None:
        operands.append(low)
        in_specs.append(pl.BlockSpec(memory_space=pl.ANY))
        aliases = {4: 0}
        kernel = lambda t, a, b, c, _, *rest: left_kernel(t, a, b, c, *rest)
    return pl.pallas_call(
        kernel,
        out_shape=outs,
        grid_spec=pltpu.PrefetchScalarGridSpec(
            num_scalar_prefetch=1,
            grid=(cols // width,),
            in_specs=in_specs,
            out_specs=(
                pl.BlockSpec((rows, width), lambda k, t: (t[0], k)),
                pl.BlockSpec((rows, rank), lambda k, t: (0, 0)),
            ),
            scratch_shapes=[pltpu.VMEM((rows, rank), F32)],
        ),
        input_output_aliases=aliases,
        cost_estimate=pl.CostEstimate(
            flops=2 * rows * cols * rank, transcendentals=0, bytes_accessed=8 * rows * cols + 2 * cols * rank
        ),
        name="left_product",
    )(*operands)


def join_kernel(place_ref, own_ref, other_ref, left_ref, left_t_ref, keep_ref, give_ref, *, parts):
    x, z, core = place_ref[0], place_ref[1], place_ref[2]
    rows, rank = left_ref.shape
    size = rows // 2 // parts
    for ref, half in ((own_ref, x), (other_ref, 1 - x)):
        for s in range(parts):
            at = pl.multiple_of(half * (rows // 2) + (z ^ s) * size, 16)
            left_ref[pl.ds(at, size), :] = ref[s * size : (s + 1) * size, :]
    left = left_ref[...]
    left_t = left.T
    left_t_ref[...] = left_t
    h, q = rank // 2, rank // 4
    first = dot(left_t[: h + q], left[:, :h], ((1,), (0,)))
    corner = dot(left_t[h:], left[:, h:], ((1,), (0,)))
    second = jnp.concatenate([corner, dot(left_t[h + q :], left[:, :h], ((1,), (0,)))])
    lower = core == 0
    keep_ref[...] = jnp.where(lower, first, second)
    give_ref[...] = jnp.where(lower, second, first)


def join_left(place, own, other, parts):
    rows, rank = 2 * own.shape[0], own.shape[1]
    pack = jax.ShapeDtypeStruct((rank // 4 * 3, rank // 2), F32)
    return pl.pallas_call(
        lambda *refs: join_kernel(*refs, parts=parts),
        out_shape=(
            jax.ShapeDtypeStruct((rows, rank), BF16),
            jax.ShapeDtypeStruct((rank, rows), BF16),
            pack,
            pack,
        ),
        in_specs=[pl.BlockSpec(memory_space=pltpu.SMEM), WHOLE, WHOLE],
        cost_estimate=pl.CostEstimate(flops=2 * rows * rank * rank, transcendentals=0, bytes_accessed=6 * rows * rank),
        compiler_params=PARAMS,
        name="join_left",
    )(place, own, other)


def right_kernel(table, left_ref, low_ref, *refs, split, sums):
    part = dot(left_ref[...], low_ref[...], ((1,), (0,)))
    step = pl.program_id(0)
    if sums:
        part = part + refs[0][...].astype(F32)
    if split == 0:
        refs[-1][...] = part.astype(refs[-1].dtype)
        return

    @pl.when(step < split)
    def _():
        refs[-2][...] = part.astype(refs[-2].dtype)

    @pl.when(step >= split)
    def _():
        refs[-1][...] = part.astype(refs[-1].dtype)


def right_product(blocks, left_t, low, dtype, split, received=None):
    rank, rows = left_t.shape
    count = blocks.shape[0]
    width = low.shape[1] // 16
    if split:
        maps = [lambda k, t: (0, jnp.minimum(k, split - 1)), lambda k, t: (0, jnp.maximum(k - split, 0))]
        shapes = [split, count - split]
    else:
        maps, shapes = [lambda k, t: (0, k)], [count]
    operands = [blocks, left_t, low]
    in_specs = [
        pl.BlockSpec((rank, rows), lambda k, t: (0, 0)),
        pl.BlockSpec((rows, width), lambda k, t: (0, t[k])),
    ]
    blocked = [pl.BlockSpec((rank, width), m) for m in maps]
    if received is not None:
        operands.append(received)
        in_specs.append(pl.BlockSpec((rank, width), lambda k, t: (0, k)))
    return pl.pallas_call(
        lambda *refs: right_kernel(*refs, split=split, sums=received is not None),
        out_shape=tuple(jax.ShapeDtypeStruct((rank, n * width), dtype) for n in shapes),
        grid_spec=pltpu.PrefetchScalarGridSpec(
            num_scalar_prefetch=1, grid=(count,), in_specs=in_specs, out_specs=tuple(blocked)
        ),
        cost_estimate=pl.CostEstimate(
            flops=2 * rank * rows * count * width,
            transcendentals=0,
            bytes_accessed=2 * count * width * (rows + 2 * rank),
        ),
        compiler_params=PARAMS,
        name="right_product",
    )(*operands)


def invert_block(block):
    size = block.shape[1]
    lane = lax.broadcasted_iota(jnp.int32, (8, size), 1)
    sub = lax.broadcasted_iota(jnp.int32, (8, size), 0)
    count = size // 8
    rows = [block[8 * v : 8 * v + 8, :] for v in range(count)]
    scales = []

    def spread(value, j):
        return jnp.broadcast_to(value[:, j : j + 1], (8, size))

    def repeat(value, k):
        return jnp.broadcast_to(value[k : k + 1, :], (8, size))

    for p in range(count):
        start = 8 * p
        inside = (lane >= start) & (lane < start + 8)
        panel = rows[p]
        columns = [spread(panel, start + k) for k in range(8)]
        panel = jnp.where(inside, 0.0, panel)
        upper, inverses, pivot_rows = {}, [], []
        scale = jnp.zeros((8, size), F32)
        for k in range(8):
            pivot = repeat(columns[k], k)
            inverse = 1.0 / pivot
            inverses.append(inverse)
            for m in range(k + 1, 8):
                upper[k, m] = repeat(columns[m], k)
            row = jnp.where(lane == start + k, 1.0, repeat(panel, k))
            pivot_rows.append(row)
            scale = jnp.where(sub == k, lax.rsqrt(pivot), scale)
            if k < 7:
                factor = jnp.where(sub > k, columns[k] * inverse, 0.0)
                panel = panel - factor * row
                for m in range(k + 1, 8):
                    columns[m] = columns[m] - factor * upper[k, m]
        rows[p] = panel
        scales.append(scale)
        for v in range(p + 1, count):
            value = rows[v]
            columns = [spread(value, start + k) for k in range(8)]
            value = jnp.where(inside, 0.0, value)
            for k in range(8):
                factor = columns[k] * inverses[k]
                value = value - factor * pivot_rows[k]
                for m in range(k + 1, 8):
                    columns[m] = columns[m] - factor * upper[k, m]
            rows[v] = value
    done = []
    for v in range(count):
        unit = jnp.where(lane == sub + 8 * v, 1.0, 0.0)
        done.append(jnp.where(lane < sub + 8 * v, rows[v], unit) * scales[v])
    return jnp.concatenate(done, 0)


def eliminate(work, out_ref, k, size):
    n = out_ref.shape[0]
    here, before = slice(k * size, (k + 1) * size), slice(0, k * size)
    upto, after = slice(0, (k + 1) * size), slice((k + 1) * size, n)
    inverse = invert_block(work[here, here])
    out_ref[here, here] = inverse
    if k > 0:
        out_ref[here, before] = dot(inverse, out_ref[here, before], ((1,), (0,)), HIGHEST)
    if (k + 1) * size < n:
        factor = dot(work[after, here], inverse, ((1,), (1,)), HIGHEST)
        work[after, after] -= dot(factor, factor, ((1,), (1,)), HIGHEST)
        out_ref[after, upto] -= dot(factor, out_ref[here, upto], ((1,), (0,)), HIGHEST)


def first_blocks_kernel(core_ref, mine_ref, other_ref, work, out_ref, *, size):
    n = out_ref.shape[0]
    h, q = n // 2, n // 4
    lower = core_ref[0] == 0
    pack0 = jnp.where(lower, mine_ref[...], other_ref[...])
    pack1 = jnp.where(lower, other_ref[...], mine_ref[...])
    diagonal = lax.broadcasted_iota(jnp.int32, (h, h), 0) == lax.broadcasted_iota(jnp.int32, (h, h), 1)
    top, bottom = pack0[:h], pack1[:h]
    trace = jnp.sum(jnp.where(diagonal, top + bottom, 0.0))
    shift = jnp.where(diagonal, ridge_scale * (trace / n), 0.0)
    work[:h, :h] = top + shift
    work[h:, h:] = bottom + shift
    work[:h, h:] = jnp.zeros((h, h), F32)
    work[h : h + q, :h] = pack0[h:]
    work[h + q :, :h] = pack1[h:]
    out_ref[...] = jnp.zeros_like(out_ref)
    for k in range(n // size // 2):
        eliminate(work, out_ref, k, size)


def last_blocks_kernel(work_in, out_in, out_ref, work, *, size):
    n = out_ref.shape[0]
    h = n // 2
    work[h:, h:] = work_in[h:, h:]
    out_ref[...] = out_in[...]
    for k in range(n // size // 2, n // size):
        eliminate(work, out_ref, k, size)


VMEM_LIMIT = 24 * 2**20
PARAMS = pltpu.CompilerParams(vmem_limit_bytes=VMEM_LIMIT)
WHOLE = pl.BlockSpec(memory_space=pltpu.VMEM)


def inverse_factor_start(core, mine, other, n):
    shape = jax.ShapeDtypeStruct((n, n), F32)
    return pl.pallas_call(
        lambda *refs: first_blocks_kernel(*refs, size=LANES),
        out_shape=(shape, shape),
        in_specs=[pl.BlockSpec(memory_space=pltpu.SMEM), WHOLE, WHOLE],
        cost_estimate=pl.CostEstimate(flops=5 * 10**9, transcendentals=0, bytes_accessed=8 * n * n),
        compiler_params=PARAMS,
        name="inverse_factor_start",
    )(core, mine, other)


def inverse_factor_end(work, partial):
    n = work.shape[0]
    return pl.pallas_call(
        lambda *refs: last_blocks_kernel(*refs, size=LANES),
        out_shape=jax.ShapeDtypeStruct((n, n), F32),
        scratch_shapes=[pltpu.VMEM((n, n), F32)],
        cost_estimate=pl.CostEstimate(flops=5 * 10**9, transcendentals=0, bytes_accessed=8 * n * n),
        compiler_params=PARAMS,
        name="inverse_factor_end",
    )(work, partial)


def finish_kernel(inverse_ref, *refs, scale):
    inverse = inverse_ref[...]
    high = inverse.astype(BF16)
    low = (inverse - high.astype(F32)).astype(BF16)
    total = jnp.zeros((inverse.shape[0], 1), F32)
    for half in range(2):
        own, near, far = (ref[...].astype(F32) for ref in refs[3 * half : 3 * half + 3])
        out_ref = refs[6 + half]
        value = ((own + near) + far) * scale
        value_high = value.astype(BF16)
        value_low = (value - value_high.astype(F32)).astype(BF16)
        piece = (
            dot(high, value_high, ((1,), (0,)))
            + dot(low, value_high, ((1,), (0,)))
            + dot(high, value_low, ((1,), (0,)))
        )
        total = total + jnp.sum(piece * piece, axis=1, keepdims=True)
        out_ref[...] = piece.astype(BF16)
    refs[8][...] = jnp.broadcast_to(total, refs[8].shape)


def finish_piece(inverse, first, second, scale):
    rank = inverse.shape[0]
    width = first[1].shape[1] // 2
    column = lambda at: pl.BlockSpec((rank, width), lambda i: (0, at))
    in_specs = [pl.BlockSpec((rank, rank), lambda i: (0, 0)), column(1), column(1), column(0)]
    in_specs += [column(3), column(1), column(0)]
    shape = jax.ShapeDtypeStruct((rank, width), BF16)
    return pl.pallas_call(
        lambda *refs: finish_kernel(*refs, scale=scale),
        grid=(1,),
        in_specs=in_specs,
        out_specs=(column(0), column(0), pl.BlockSpec((rank, LANES), lambda i: (0, 0))),
        out_shape=(shape, shape, jax.ShapeDtypeStruct((rank, LANES), F32)),
        cost_estimate=pl.CostEstimate(flops=12 * rank * rank * width, transcendentals=0, bytes_accessed=20 * rank * width),
        compiler_params=PARAMS,
        name="finish_piece",
    )(inverse, *first, *second)


def orthonormal_kernel(left_ref, inverse_ref, out_ref):
    inverse = inverse_ref[...]
    high = inverse.astype(BF16)
    low = (inverse - high.astype(F32)).astype(BF16)
    left = left_ref[...]
    out_ref[...] = (dot(left, high, ((1,), (1,))) + dot(left, low, ((1,), (1,)))).astype(BF16)


def orthonormal_rows(left, inverse):
    return pl.pallas_call(
        orthonormal_kernel,
        out_shape=jax.ShapeDtypeStruct(left.shape, BF16),
        cost_estimate=pl.CostEstimate(flops=4 * left.size * inverse.shape[0], transcendentals=0, bytes_accessed=4 * left.size),
        compiler_params=PARAMS,
        name="orthonormal_rows",
    )(left, inverse)


def momentum_kernel(table, ortho_ref, mom_ref, grad_ref, *refs, count):
    pieces, mom_out, right = refs[:count], refs[-2], refs[-1]
    for i in range(count):

        @pl.when(pl.program_id(0) == i)
        def _(i=i):
            right[...] = pieces[i][...]

    feedback = dot(ortho_ref[...], right[...], ((1,), (0,)))
    mom_out[0] = mom_ref[0] + grad_ref[0].astype(F32) - (1 - momentum_decay) * feedback


def write_momentum(blocks, ortho, momentum, gradients, pieces, previous):
    _, rows, cols = momentum.shape
    rank, width = pieces[0].shape
    count = len(pieces)
    whole = lambda k, t: (0, 0)
    local = pl.BlockSpec((1, rows, width), lambda k, t: (0, 0, t[k]))
    operands = [blocks, ortho, momentum, gradients, *pieces]
    in_specs = [pl.BlockSpec((rows, rank), whole), local, local] + [pl.BlockSpec((rank, width), whole)] * count
    aliases = {}
    if previous is not None:
        aliases = {len(operands): 0}
        operands.append(previous)
        in_specs.append(pl.BlockSpec(memory_space=pl.ANY))
    return pl.pallas_call(
        lambda *refs: momentum_kernel(*refs, count=count),
        out_shape=jax.ShapeDtypeStruct((1, rows, cols), F32),
        grid_spec=pltpu.PrefetchScalarGridSpec(
            num_scalar_prefetch=1,
            grid=(count,),
            in_specs=in_specs,
            out_specs=local,
            scratch_shapes=[pltpu.VMEM((rank, width), BF16)],
        ),
        input_output_aliases=aliases,
        cost_estimate=pl.CostEstimate(
            flops=2 * rows * rank * width * count, transcendentals=0, bytes_accessed=10 * rows * width * count
        ),
        compiler_params=PARAMS,
        name="write_momentum",
    )(*operands)


def update_kernel(table, rms_ref, ortho_ref, *refs, count, scale):
    pieces, (basis_out, update_out, right) = refs[:count], refs[-3:]
    for i in range(count):

        @pl.when(pl.program_id(0) == i)
        def _(i=i):
            right[...] = (pieces[i][...].astype(F32) / rms_ref[:, :1]).astype(BF16)

    basis = right[...]
    basis_out[...] = basis.T
    update_out[...] = (scale * dot(ortho_ref[...], basis, ((1,), (0,)))).astype(BF16)


def write_update(blocks, rms, ortho, pieces, scale, cols, previous):
    rows = ortho.shape[0]
    rank, width = pieces[0].shape
    count = len(pieces)
    whole = lambda k, t: (0, 0)
    operands = [blocks, rms, ortho, *pieces]
    in_specs = [pl.BlockSpec((rank, LANES), whole), pl.BlockSpec((rows, rank), whole)]
    in_specs += [pl.BlockSpec((rank, width), whole)] * count
    aliases = {}
    if previous is not None:
        aliases = {len(operands) + i: i for i in range(2)}
        operands += list(previous)
        in_specs += [pl.BlockSpec(memory_space=pl.ANY)] * 2
    return pl.pallas_call(
        lambda *refs: update_kernel(*refs, count=count, scale=scale),
        out_shape=(jax.ShapeDtypeStruct((cols, rank), BF16), jax.ShapeDtypeStruct((rows, cols), BF16)),
        grid_spec=pltpu.PrefetchScalarGridSpec(
            num_scalar_prefetch=1,
            grid=(count,),
            in_specs=in_specs,
            out_specs=(
                pl.BlockSpec((width, rank), lambda k, t: (t[k], 0)),
                pl.BlockSpec((rows, width), lambda k, t: (0, t[k])),
            ),
            scratch_shapes=[pltpu.VMEM((rank, width), BF16)],
        ),
        input_output_aliases=aliases,
        cost_estimate=pl.CostEstimate(
            flops=2 * rows * rank * width * count,
            transcendentals=0,
            bytes_accessed=2 * width * count * (rows + 2 * rank),
        ),
        compiler_params=PARAMS,
        name="write_update",
    )(*operands)


def by_pieces(gradients, momentum, right_basis):
    _, local_rows, local_cols = momentum.shape
    rank = right_basis.shape[1]
    groups, cols = lax.axis_size("grp"), lax.axis_size("col")
    model_rows = local_rows * lax.axis_size("row")
    model_cols = local_cols * cols
    x, row, z = lax.axis_index("grp"), lax.axis_index("row"), lax.axis_index("col")
    y, core = row // 2, row % 2

    theirs = jnp.reshape(1 - x, (1,)).astype(jnp.int32)
    mine = jnp.reshape(x, (1,)).astype(jnp.int32)
    low, left_theirs = left_product(theirs, gradients, momentum, right_basis, BF16)
    left_from_x = swap(left_theirs, "grp", 1)
    low, left_mine = left_product(mine, gradients, momentum, right_basis, F32, low)
    half = (left_mine + left_from_x.astype(F32)).reshape(cols, -1, rank)
    pick = lambda s: lax.dynamic_index_in_dim(half, z ^ s, 0, keepdims=False)
    piece = pick(0)
    for s in range(1, cols):
        piece = piece + swap(pick(s).astype(BF16), "col", s).astype(F32)
    piece = piece.astype(BF16)
    half = jnp.concatenate([piece] + [swap(piece, "col", s) for s in range(1, cols)])
    other = swap(half, "grp", 1)
    place = jnp.stack([x, z, core]).astype(jnp.int32)
    left, left_t, keep, give = join_left(place, half, other, cols)

    def block(part, dc, dx, dy):
        return ((core ^ dc) * 4 + (x ^ dx) * 2 + (y ^ dy)) * 2 + part

    def table(items):
        return jnp.stack([block(*item) for item in items]).astype(jnp.int32)

    def urgent(dc):
        return table([(0, dc, 1, 1), (0, dc, 1, 0), (1, dc, 1, 1), (1, dc, 0, 1)])

    def others(dc):
        return table([(0, dc, 0, 1), (0, dc, 0, 0), (1, dc, 1, 0), (1, dc, 0, 0)])

    keep = keep + swap(give, "row", 1)
    give_urgent = right_product(urgent(1), left_t, low, BF16, 0)[0]
    got_urgent = swap(give_urgent, "row", 1)
    gram_y = swap(keep, "row", 2)
    give_others = right_product(others(1), left_t, low, BF16, 0)[0]
    got_others = swap(give_others, "row", 1)
    for_x, for_y = right_product(urgent(0), left_t, low, BF16, 2, got_urgent)
    from_x, from_y = swap(for_x, "grp", 1), swap(for_y, "row", 2)
    keep = keep + gram_y
    got = swap(keep, "row", 1)
    rest = right_product(others(0), left_t, low, F32, 0, got_others)[0]
    work, partial = inverse_factor_start(place[2:], keep, got, rank)
    width = local_cols // 16
    first_y = (rest[:, :width] + from_x[:, :width].astype(F32)).astype(BF16)
    second_x = (rest[:, 2 * width : 3 * width] + from_y[:, :width].astype(F32)).astype(BF16)
    far_y, far_x = swap(first_y, "row", 2), swap(second_x, "grp", 1)
    inverse = inverse_factor_end(work, partial)
    part_a, part_b, squares = finish_piece(inverse, (rest, from_x, far_y), (rest, from_y, far_x), 1.0 / groups)

    b_x, a_y = swap(part_b, "grp", 1), swap(part_a, "row", 2)
    a_c, b_c = swap(part_a, "row", 1), swap(part_b, "row", 1)
    a_x, b_y = swap(part_a, "grp", 1), swap(part_b, "row", 2)
    squares = squares[:, 0]
    for axis, bits in (("col", (1, 2)), ("grp", (1,)), ("row", (2, 1))):
        for bit in bits:
            squares = squares + swap(squares, axis, bit)
    column_rms = jnp.sqrt(squares / model_cols + epsilon)
    rms = jnp.broadcast_to(column_rms[:, None], (rank, LANES))
    ortho = orthonormal_rows(left, inverse)
    a_d, b_d = swap(a_y, "grp", 1), swap(b_x, "row", 2)
    scale = math.sqrt(model_rows / rank)
    groups_of_pieces = [
        ([part_a, part_b, a_c, b_c], [(0, 0, 0, 0), (1, 0, 0, 0), (0, 1, 0, 0), (1, 1, 0, 0)]),
        ([b_x, a_y, swap(b_x, "row", 1), swap(a_y, "row", 1)], [(1, 0, 1, 0), (0, 0, 0, 1), (1, 1, 1, 0), (0, 1, 0, 1)]),
        ([a_x, b_y, swap(a_x, "row", 1), swap(b_y, "row", 1)], [(0, 0, 1, 0), (1, 0, 0, 1), (0, 1, 1, 0), (1, 1, 0, 1)]),
        ([a_d, b_d, swap(a_d, "row", 1), swap(b_d, "row", 1)], [(0, 0, 1, 1), (1, 0, 1, 1), (0, 1, 1, 1), (1, 1, 1, 1)]),
    ]
    new_momentum, others_out = None, None
    for pieces, items in groups_of_pieces:
        new_momentum = write_momentum(table(items), ortho, momentum, gradients, pieces, new_momentum)
        others_out = write_update(table(items), rms, ortho, pieces, scale, local_cols, others_out)
    return (new_momentum, *others_out)


def by_collectives(gradients, momentum, right_basis):
    merged = momentum[0] + gradients[0].astype(F32)
    merged_low = merged.astype(BF16)
    rank = right_basis.shape[1]
    local_rows, local_cols = merged.shape
    model_rows = local_rows * lax.axis_size("row")
    model_cols = local_cols * lax.axis_size("col")
    groups = lax.axis_size("grp")
    left_factor = jnp.dot(merged_low, right_basis, preferred_element_type=F32)
    left_factor = lax.psum(left_factor, ("grp", "col"))
    gram_matrix = dot(left_factor, left_factor, ((0,), (0,)), HIGHEST)
    gram_matrix = lax.psum(gram_matrix, "row")
    shifted = gram_matrix + ridge_scale * (jnp.trace(gram_matrix) / rank) * jnp.eye(rank, dtype=F32)
    cholesky_factor = jnp.linalg.cholesky(shifted)
    orthonormal = jax.scipy.linalg.solve_triangular(cholesky_factor, left_factor.T, lower=True).T
    orthonormal_low = orthonormal.astype(BF16)
    right_piece = lax.psum_scatter(
        jnp.einsum("ij,ik->jk", merged_low, orthonormal_low, preferred_element_type=F32) / groups,
        ("grp", "row"),
        scatter_dimension=0,
        tiled=True,
    )
    squares_sum = lax.psum(jnp.sum(right_piece * right_piece, axis=0), ("grp", "row", "col"))
    column_rms = jnp.sqrt(squares_sum / model_cols + epsilon)
    basis_piece = (right_piece / column_rms).astype(BF16)
    new_basis = lax.all_gather(basis_piece, ("grp", "row"), axis=0, tiled=True)
    scaled_low = (orthonormal * column_rms).astype(BF16)
    stacked_left = jnp.concatenate([orthonormal_low, scaled_low], axis=0)
    products = dot(stacked_left, new_basis, ((1,), (1,)))
    update = (math.sqrt(model_rows / rank) * products[:local_rows]).astype(BF16)
    new_momentum = merged - (1 - momentum_decay) * products[local_rows:]
    return (new_momentum[None], new_basis, update)


def solution(mesh):
    placed = (P("grp", "row", "col"), P("grp", "row", "col"), P("col", None))

    def per_device(gradients, momentum, right_basis):
        _, rows, cols = momentum.shape
        rank = right_basis.shape[1]
        fits = (
            mesh.shape["grp"] == 2
            and mesh.shape["row"] == 4
            and mesh.shape["col"] == 4
            and rows % LANES == 0
            and cols % (16 * LANES) == 0
            and cols % 512 == 0
            and rank % (4 * LANES) == 0
        )
        return (by_pieces if fits else by_collectives)(gradients, momentum, right_basis)

    return jax.shard_map(
        per_device,
        mesh=mesh,
        in_specs=placed,
        out_specs=(P("grp", "row", "col"), P("col", None), P("row", "col")),
        check_vma=False,
    )
```
